32 devices in a mesh: section: 4 (over y, core), expert: 8 (over z, x).
Axes of the slice: x: 2, y: 2, z: 4, core: 2. Of those that a mesh axis runs over, the one named last changes fastest.
Arguments:
- token_ids: int32 [4, 128], replicated, may hold values from 0 to 75967
- embed_table: bfloat16 [75968, 2048], P('section', 'expert'), may hold values from -6 to 6
- attn_gain: float32 [4, 2048], P('section'), may hold values from 0.5 to 1.5
- moe_gain: float32 [4, 2048], P('section'), may hold values from 0.5 to 1.5
- query_gain: float32 [4, 32, 128], P('section'), may hold values from 0.1 to 1.9
- key_gain: float32 [4, 2, 128], P('section'), may hold values from 0.1 to 1.9
- key_cache: bfloat16 [4, 128, 128, 256], P('section', 'expert'), may hold values from -210 to 210
- value_cache: bfloat16 [4, 128, 128, 256], P('section', 'expert'), may hold values from -3 to 3
- cache_len: int32 [128], P('expert'), may hold values from 1 to 128, 8192 in all
- expert_ids: int32 [4, 4, 128, 4], P('section'), may hold values from 0 to 7, all different within a row; in each aligned block of 4 rows (0 to 3, 4 to 7, ..., all dimensions but the last counted through in order) at most 4 rows name the same one
- route_raw: float32 [4, 4, 128, 4], P('section'), may hold values from 0.1 to 1
- gate_weights: bfloat16 [4, 8, 2048, 768], P('section', 'expert'), may hold values from -0.125 to 0.125
- up_weights: bfloat16 [4, 8, 2048, 768], P('section', 'expert'), may hold values from -0.125 to 0.125
- down_weights: bfloat16 [4, 8, 768, 2048], P('section', 'expert'), may hold values from -0.21875 to 0.21875
Outputs:
- hidden: bfloat16 [4, 4, 128, 2048], P('section', None, 'expert')
The draws below stay inside these ranges and needn't reach their ends.
Inputs may be any that keep to these rules, and one draw needn't show every extreme that they name: `expert_ids`: in each layer and step, at most 4 of the rows of one aligned block of 4 rows name one expert, a bound that some block reaches of them. `cache_len`: some row holds 128 entries.
All inputs are finite; a program needn't handle non-finite values. No bound on the sum of `cache_len` on one device may be relied on, other than what follows from the above.
Results may differ from the reference program's by a relative error of at most 0.02.
Values may be sent and summed in bfloat16 or wider, within the bound.
A program may use at most 64 MiB of HBM per device.

```python
import math
import jax
import jax.numpy as jnp
import numpy as np
from jax import lax

D = 2048
FF = 768
HD = 128
KVH = 2
VOCAB = 75968
QH = 32
BLOCK = 4
CACHE = 128
STEPS = 4
EXPERTS = 8
TOPK = 4
CAP = 4
ROWS = 128
LAYERS = 4


def draw_key_cache(key, part):
    shape = (LAYERS, ROWS, CACHE, KVH * HD)
    return jnp.clip(jax.random.normal(key, shape, jnp.float32), -6.0, 6.0).astype(jnp.bfloat16)


def touch_ends(result, rng, low, largest):
    index_at = [jax.random.randint(jax.random.fold_in(rng, axis), (), 0, length) for axis, length in enumerate(result.shape)]
    longest = result.shape.index(max(result.shape))
    beside = index_at[:longest] + [(index_at[longest] + 1) % result.shape[longest]] + index_at[longest + 1:]
    return result.at[tuple(index_at)].set(low).at[tuple(beside)].set(largest)


def levels(stream_key, shape, cuts, least, top_value):
    def one(dim, blocks):
        draws = jax.random.uniform(jax.random.fold_in(jax.random.fold_in(stream_key, 6), dim), (blocks,), jnp.float32, least / len(cuts), top_value / len(cuts))
        return jnp.repeat(jnp.exp(draws), shape[dim] // blocks).reshape((-1,) + (1,) * (len(shape) - dim - 1))

    loudness = one(*cuts[0])
    for cut in cuts[1:]:
        loudness = loudness * one(*cut)
    return loudness


def profile(number_of, total, most, lean):
    loads = [(1 << 20) // math.isqrt(grade ** lean) + 1 for grade in range(2, number_of + 1)]
    rest, given = total - most - (number_of - 1), [1] * (number_of - 1)
    while rest > 0:
        movable = [i for i in range(number_of - 1) if given[i] < most]
        whole, budget = sum([loads[i] for i in movable]), rest
        for i in movable:
            more = min(most - given[i], max(1, budget * loads[i] // whole), rest)
            given[i] = given[i] + more
            rest = rest - more
    return np.array([most] + given)


def ragged_sizes(rng, count, total, most, lean):
    if count == 2:
        one = jax.random.randint(rng, (), max(1, total - most), min(most, total - 1) + 1)
        return jnp.stack([one, total - one])
    tallies = jnp.asarray(profile(count, total, most, lean), jnp.int32)
    twos = (count - 1) // 2
    giver, receiver = tallies[1:1 + 2 * twos:2], tallies[2:2 + 2 * twos:2]
    room = jnp.minimum(giver - 1, most - receiver)
    moved = jax.random.randint(jax.random.fold_in(rng, 1), (twos,), 0, 1 << 20) % (room + 1)
    tallies = tallies.at[1:1 + 2 * twos:2].set(giver - moved).at[2:2 + 2 * twos:2].set(receiver + moved)
    return tallies[jax.random.permutation(jax.random.fold_in(rng, 2), count)]


def shared_out(rng, own, number, rows, number_of, top, most, lean):
    order = jax.random.permutation(rng, number_of)
    heavy_load, ordinary = portions_of(number_of, rows * top, most, lean, True), portions_of(number_of, rows * top, most, lean, False)
    places = jnp.arange(number_of)

    def named(sizes, offset_by):
        used = int((sizes > 0).sum())
        fixed = max(1, used // 4)
        moved = fixed + (places - fixed + offset_by * (used - fixed)) % max(1, number_of - fixed)
        return jnp.zeros((number_of,), jnp.int32).at[order[jnp.where(places < fixed, places, moved)]].set(jnp.asarray(sizes, jnp.int32))

    sizes = jnp.where(number % 4 == 0, named(heavy_load, number // 4), named(ordinary, number - number // 4 - 1))
    mixed = jax.random.permutation(jax.random.fold_in(own, 3), number_of)
    giver, sink = mixed[0:number_of // 2 * 2:2], mixed[1:number_of // 2 * 2:2]
    slack = jnp.minimum(sizes[giver] - 1, most - sizes[sink]) // 2
    slack = jnp.where((giver == order[0]) | (sink == order[0]) | (sizes[sink] == 0), 0, jnp.maximum(slack, 0))
    moved = jax.random.randint(jax.random.fold_in(own, 4), (number_of // 2,), 0, 1 << 20) % (slack + 1)
    sizes = sizes.at[giver].add(-moved).at[sink].add(moved)
    items = jnp.searchsorted(jnp.cumsum(sizes), jnp.arange(rows * top), side="right").astype(jnp.int32)
    table = items.reshape(top, rows).T
    table = table[jax.random.permutation(jax.random.fold_in(own, 1), rows)]
    offset_by = jax.random.randint(jax.random.fold_in(own, 2), (rows, 1), 0, top)
    return jnp.take_along_axis(table, (jnp.arange(top)[None, :] + offset_by) % top, axis=1)


def portions_of(amount, total, most, skew, full):
    portions = [(1 << 20) // math.isqrt(grade ** skew) + 1 for grade in range(1, amount + 1)]
    largest = most if full else min(most, max(-(-total // amount), total * portions[0] // sum(portions)))
    least = 1 if total - largest >= amount - 1 else 0
    holding, surplus = [largest] + [least] * (amount - 1), total - largest - least * (amount - 1)
    while surplus > 0:
        candidates = [i for i in range(1, amount) if holding[i] < largest] or [i for i in range(1, amount) if holding[i] < most]
        pool, left = sum([portions[i] for i in candidates]), surplus
        for i in candidates:
            extra = min(most - holding[i], max(1, left * portions[i] // pool), surplus)
            holding[i] = holding[i] + extra
            surplus = surplus - extra
    return np.array(holding)


def gaussian(stream_key, extent, width, bound, cuts=(), kind=jnp.bfloat16):
    array = jax.random.normal(stream_key, extent, jnp.float32) * width
    if len(cuts) > 0:
        array = levels(stream_key, extent, cuts, -0.22, 0.18) * array
    return jnp.clip(array, min=-bound, max=bound).astype(kind)


def setup_inputs(seed: int = 0) -> dict:
    key_list = jax.random.split(jax.random.key(seed), 15)
    token_ids = touch_ends(jax.random.randint(key_list[0], (STEPS, ROWS), 0, VOCAB), jax.random.fold_in(key_list[0], 1), 0, VOCAB - 1).astype(jnp.int32)
    embed_table = gaussian(key_list[1], (VOCAB, D), 1.0, 6.0, ((0, 4), (1, 8)))
    attn_gain = jnp.clip(1.0 + 0.1 * jax.random.normal(key_list[2], (LAYERS, D), jnp.float32), 0.5, 1.5)
    moe_gain = jnp.clip(1.0 + 0.1 * jax.random.normal(key_list[3], (LAYERS, D), jnp.float32), 0.5, 1.5)
    query_gain = jnp.clip(1.0 + 0.18 * jax.random.normal(key_list[4], (LAYERS, QH, HD), jnp.float32), 0.1, 1.9)
    key_gain = jnp.clip(1.0 + 0.18 * jax.random.normal(key_list[5], (LAYERS, KVH, HD), jnp.float32), 0.1, 1.9)
    key_cache = draw_key_cache(jax.random.fold_in(key_list[14], 71), 0)
    value_cache = gaussian(key_list[7], (LAYERS, ROWS, CACHE, KVH * HD), 0.5, 3.0, ((0, 4), (1, 8)))
    cache_len = ragged_sizes(key_list[8], ROWS, ROWS * CACHE // 2, CACHE, 2).astype(jnp.int32)
    expert_ids_keys = jax.random.split(jax.random.fold_in(key_list[9], 1), LAYERS * STEPS * ROWS // BLOCK)
    expert_ids_turns = jax.random.permutation(jax.random.fold_in(key_list[9], 3), LAYERS * STEPS * ROWS // BLOCK)
    expert_ids = jax.vmap(lambda own, number: shared_out(jax.random.fold_in(key_list[9], 2), own, number, BLOCK, EXPERTS, TOPK, CAP, 2))(expert_ids_keys, expert_ids_turns).reshape((LAYERS, STEPS, ROWS, TOPK))
    route_raw = jnp.clip(jnp.exp(math.log(1.0) - 2.3025851 * jax.random.uniform(key_list[10], (LAYERS, STEPS, ROWS, TOPK), jnp.float32) ** levels(key_list[10], (LAYERS, STEPS, ROWS, TOPK), ((0, 4),), -0.2, 0.2)), 0.1, 1.0)
    gate_weights = gaussian(key_list[11], (LAYERS, EXPERTS, D, FF), D ** -0.5, 0.125, ((0, 4), (1, 8)))
    up_weights = gaussian(key_list[12], (LAYERS, EXPERTS, D, FF), D ** -0.5, 0.125, ((0, 4), (1, 8)))
    down_weights = gaussian(key_list[13], (LAYERS, EXPERTS, FF, D), FF ** -0.5, 0.21875, ((0, 4), (1, 8)))
    return {"token_ids": token_ids, "embed_table": embed_table, "attn_gain": attn_gain, "moe_gain": moe_gain, "query_gain": query_gain, "key_gain": key_gain, "key_cache": key_cache, "value_cache": value_cache, "cache_len": cache_len, "expert_ids": expert_ids, "route_raw": route_raw, "gate_weights": gate_weights, "up_weights": up_weights, "down_weights": down_weights}


eps = 1e-06

def rms_scale(values):
    return lax.rsqrt(lax.optimization_barrier(jnp.mean(values * values, axis=-1, keepdims=True)) + eps)

def attend(queries, key_rows, value_rows, near_keys, near_values, lengths, step_at):
    row_count = queries.shape[0]
    score_scale = 1.0 / math.sqrt(HD)
    key_grid = key_rows.reshape(row_count, CACHE, KVH, HD).astype(jnp.float32)
    value_grid = value_rows.reshape(row_count, CACHE, KVH, HD).astype(jnp.float32)
    near_key_grid = near_keys.reshape(STEPS, row_count, KVH, HD).astype(jnp.float32)
    near_value_grid = near_values.reshape(STEPS, row_count, KVH, HD).astype(jnp.float32)
    query_wide = queries.astype(jnp.float32)
    far_scores = jnp.einsum('rgjd,rcgd->rgjc', query_wide, key_grid) * score_scale
    near_scores = jnp.einsum('rgjd,srgd->rgjs', query_wide, near_key_grid) * score_scale
    far_allowed = (jnp.arange(CACHE)[None, :] < lengths[:, None])[:, None, None, :]
    near_allowed = (jnp.arange(STEPS) <= step_at)[None, None, None, :]
    far_scores = jnp.where(far_allowed, far_scores, -1e+30)
    near_scores = jnp.where(near_allowed, near_scores, -1e+30)
    row_top = jnp.maximum(lax.optimization_barrier(jnp.max(far_scores, axis=-1, keepdims=True)), lax.optimization_barrier(jnp.max(near_scores, axis=-1, keepdims=True)))
    far_exp = jnp.where(far_allowed, jnp.exp(far_scores - row_top), 0.0)
    near_exp = jnp.where(near_allowed, jnp.exp(near_scores - row_top), 0.0)
    denominator = lax.optimization_barrier(jnp.sum(far_exp, axis=-1, keepdims=True)) + lax.optimization_barrier(jnp.sum(near_exp, axis=-1, keepdims=True))
    far_probs = (far_exp / denominator).astype(jnp.bfloat16).astype(jnp.float32)
    near_probs = (near_exp / denominator).astype(jnp.bfloat16).astype(jnp.float32)
    return jnp.einsum('rgjc,rcgd->rgjd', far_probs, value_grid) + jnp.einsum('rgjs,srgd->rgjd', near_probs, near_value_grid)

def expert_mix(routed, chosen_ids, raw_weights, gate_layer, up_layer, down_layer):
    row_count = routed.shape[0]
    weights = raw_weights / lax.optimization_barrier(jnp.sum(raw_weights, axis=-1, keepdims=True))
    limit = min(row_count, row_count // BLOCK * CAP)

    def one_expert(expert_at):
        matches = chosen_ids == expert_at
        member = jnp.any(matches, axis=-1)
        shares = lax.optimization_barrier(jnp.sum(jnp.where(matches, weights, 0.0), axis=-1))
        picked = jnp.nonzero(member, size=limit, fill_value=0)[0].astype(jnp.int32)
        live = jnp.arange(limit) < jnp.sum(member.astype(jnp.int32))
        rows_in = routed[picked]
        gate_part = jnp.dot(rows_in, gate_layer[expert_at], preferred_element_type=jnp.float32)
        lifted = jnp.dot(rows_in, up_layer[expert_at], preferred_element_type=jnp.float32)
        activated = (jax.nn.silu(gate_part) * lifted).astype(jnp.bfloat16)
        expert_out = jnp.dot(activated, down_layer[expert_at], preferred_element_type=jnp.float32).astype(jnp.bfloat16)
        factor = jnp.where(live, shares[picked], 0.0)
        return (picked, factor[:, None] * expert_out)
    picked_all, terms = lax.map(one_expert, jnp.arange(EXPERTS, dtype=jnp.int32))
    mixture = jnp.zeros((row_count, D), jnp.float32)
    return mixture.at[picked_all.reshape(-1)].add(terms.reshape(-1, D))

def reference(token_ids, embed_table, attn_gain, moe_gain, query_gain, key_gain, key_cache, value_cache, cache_len, expert_ids, route_raw, gate_weights, up_weights, down_weights):
    blocks = D // HD
    embedded = jnp.take(embed_table, token_ids, axis=0)
    fresh_keys = jnp.zeros((LAYERS, STEPS, ROWS, KVH * HD), jnp.bfloat16)
    fresh_values = jnp.zeros((LAYERS, STEPS, ROWS, KVH * HD), jnp.bfloat16)
    per_step = []
    for step_at in range(STEPS):
        hidden_now = embedded[step_at]
        per_layer = []
        for layer_at in range(LAYERS):
            hidden_wide = hidden_now.astype(jnp.float32)
            scaled = hidden_wide * rms_scale(hidden_wide) * attn_gain[layer_at]
            pieces = scaled.reshape(ROWS, blocks, HD)
            normed = pieces * rms_scale(pieces)
            queries = (normed[:, None] * query_gain[layer_at].reshape(KVH, blocks, HD)).astype(jnp.bfloat16)
            key_new = (normed[:, :KVH] * key_gain[layer_at]).astype(jnp.bfloat16).reshape(ROWS, KVH * HD)
            value_new = pieces[:, KVH:2 * KVH].astype(jnp.bfloat16).reshape(ROWS, KVH * HD)
            fresh_keys = fresh_keys.at[layer_at, step_at].set(key_new)
            fresh_values = fresh_values.at[layer_at, step_at].set(value_new)
            head_out = attend(queries, key_cache[layer_at], value_cache[layer_at], fresh_keys[layer_at], fresh_values[layer_at], cache_len, step_at)
            mid = hidden_wide + lax.optimization_barrier(jnp.sum(head_out, axis=1)).reshape(ROWS, D)
            routed = (mid * rms_scale(mid) * moe_gain[layer_at]).astype(jnp.bfloat16)
            mixture = expert_mix(routed, expert_ids[layer_at, step_at], route_raw[layer_at, step_at], gate_weights[layer_at], up_weights[layer_at], down_weights[layer_at])
            hidden_now = (mid + mixture).astype(jnp.bfloat16)
            per_layer.append(hidden_now)
        per_step.append(jnp.stack(per_layer))
    return jnp.stack(per_step, axis=1)
```

```python
import functools
import math

import jax
import jax.numpy as jnp
from jax import lax
from jax.experimental import pallas as pl
from jax.experimental.pallas import tpu as pltpu
from jax.sharding import PartitionSpec as P

GROUPS = 1
EPS = 1e-06
NEG = -1e30
MESH = pl.DeviceIdType.MESH
F32 = jnp.float32
BF16 = jnp.bfloat16


def layers_kernel(
    n_sec, n_exp, n_groups, dims,
    looked, far_live, shares, attn_gain, moe_gain, query_gain, key_gain,
    keys_hbm, values_hbm, gate_hbm, up_hbm, down_hbm,
    out,
    keys, values, gate, up, down,
    emb_land, h_in, near_k, near_v, qn, att, mid,
    x_land, act, y, p_land, q_land,
    load_sem, emb_send, emb_recv, h_send, h_recv,
    ag_send, fwd_send, ag_recv, p_send, p_recv, q_send, q_recv,
):
    rows, steps, width, head, kv, blocks, ff = dims
    part = width // n_exp
    nz = n_exp // 2
    per = steps // n_groups
    count = per * rows
    total = 2 * nz * count
    sec = lax.axis_index("section")
    me = lax.axis_index("expert")
    z, x = me // 2, me % 2
    partner = z * 2 + (1 - x)
    last = n_sec - 1

    loads = [
        pltpu.make_async_copy(src, dst, load_sem.at[i])
        for i, (src, dst) in enumerate(
            [(keys_hbm, keys), (values_hbm, values), (gate_hbm, gate), (up_hbm, up), (down_hbm, down)]
        )
    ]
    for load in loads:
        load.start()

    def peer(k):
        return lax.rem(z + k, nz)

    barrier = pltpu.get_barrier_semaphore()

    def greet(section, expert):
        pl.semaphore_signal(
            barrier, inc=1, device_id={"section": section, "expert": expert}, device_id_type=MESH
        )

    for k in range(1, nz):
        greet(sec, peer(k) * 2 + x)
    greet(sec, partner)

    @pl.when(sec > 0)
    def _():
        greet(sec - 1, me)
        for k in range(n_exp):
            greet(0, k)

    @pl.when(sec < last)
    def _():
        greet(sec + 1, me)

    @pl.when(sec == 0)
    def _():
        for k in range(1, n_exp):
            greet(0, lax.rem(me + k, n_exp))
        for s in range(1, n_sec):
            for k in range(n_exp):
                greet(s, k)

    @pl.when(sec == 0)
    def _():
        pl.semaphore_wait(barrier, nz + n_exp * n_sec)

    @pl.when((sec > 0) & (sec < last))
    def _():
        pl.semaphore_wait(barrier, nz + n_exp + 2)

    @pl.when(sec == last)
    def _():
        pl.semaphore_wait(barrier, nz + n_exp + 1)

    def emb_copy(k):
        to = lax.rem(me + k, n_exp)
        return pltpu.make_async_remote_copy(
            src_ref=looked.at[to], dst_ref=emb_land.at[sec, me],
            send_sem=emb_send, recv_sem=emb_recv,
            device_id={"section": 0, "expert": to}, device_id_type=MESH,
        )

    for k in range(1, n_exp):
        emb_copy(k).start()

    @pl.when(sec > 0)
    def _():
        emb_copy(0).start()

    near_k[...] = jnp.zeros_like(near_k)
    near_v[...] = jnp.zeros_like(near_v)

    @pl.when(sec == 0)
    def _():
        own = pltpu.make_async_copy(looked.at[me], emb_land.at[0, me], emb_recv)
        own.start()
        pltpu.make_async_copy(emb_land, emb_land, emb_recv).wait()
        for g in range(n_groups):
            for e in range(n_exp):
                whole = emb_land[0, e, g * count:(g + 1) * count, :].astype(F32)
                for s in range(1, n_sec):
                    whole = whole + emb_land[s, e, g * count:(g + 1) * count, :].astype(F32)
                h_in[g, :, e * part:(e + 1) * part] = whole.astype(BF16)

    def h_copy(g):
        return pltpu.make_async_remote_copy(
            src_ref=out.at[g], dst_ref=h_in.at[g],
            send_sem=h_send.at[g], recv_sem=h_recv.at[g],
            device_id={"section": sec + 1, "expert": me}, device_id_type=MESH,
        )

    def ag_copy(g, k):
        return pltpu.make_async_remote_copy(
            src_ref=x_land.at[g, 0, z], dst_ref=x_land.at[g, 0, z],
            send_sem=ag_send.at[g, k], recv_sem=ag_recv.at[g, 0, z],
            device_id={"section": sec, "expert": peer(k) * 2 + x}, device_id_type=MESH,
        )

    def fwd_copy(g, k):
        at = peer(k)
        return pltpu.make_async_remote_copy(
            src_ref=x_land.at[g, 0, at], dst_ref=x_land.at[g, 1, at],
            send_sem=fwd_send.at[g, k], recv_sem=ag_recv.at[g, 1, at],
            device_id={"section": sec, "expert": partner}, device_id_type=MESH,
        )

    def p_copy(g, k):
        at = peer(k)
        return pltpu.make_async_remote_copy(
            src_ref=y.at[g, 1, at], dst_ref=p_land.at[g, at],
            send_sem=p_send.at[g, k], recv_sem=p_recv.at[g, at],
            device_id={"section": sec, "expert": partner}, device_id_type=MESH,
        )

    def q_copy(g, k):
        at = peer(k)
        return pltpu.make_async_remote_copy(
            src_ref=y.at[g, 0, at], dst_ref=q_land.at[g, z],
            send_sem=q_send.at[g, k], recv_sem=q_recv.at[g, z],
            device_id={"section": sec, "expert": at * 2 + x}, device_id_type=MESH,
        )

    def landed(ref, sem):
        pltpu.make_async_copy(ref, ref, sem).wait()

    def cut(j, size=head):
        return slice(j * size, (j + 1) * size)

    scale = 1.0 / math.sqrt(head)
    contract = (((1,), (1,)), ((), ()))
    q_rows = per * blocks

    for g in range(n_groups):
        @pl.when(sec > 0)
        def _():
            landed(h_in.at[g], h_recv.at[g])

        square = jnp.zeros((count, head), F32)
        for j in range(blocks):
            piece = h_in[g, :, cut(j)].astype(F32)
            square = square + piece * piece
        factor = lax.rsqrt(jnp.sum(square, axis=-1, keepdims=True) / width + EPS)
        for j in range(blocks):
            piece = h_in[g, :, cut(j)].astype(F32) * factor * attn_gain[:, cut(j)]
            normed = piece * lax.rsqrt(jnp.mean(piece * piece, axis=-1, keepdims=True) + EPS)
            qn[pl.ds(j, count, stride=blocks), :] = normed
            here = slice(g * count, (g + 1) * count)
            if j < kv:
                near_k[here, cut(j)] = (normed * key_gain[j:j + 1, :]).astype(BF16)
            elif j < 2 * kv:
                near_v[here, cut(j - kv)] = piece.astype(BF16)

        if g == 0:
            loads[0].wait()
            loads[1].wait()

        spot = lax.broadcasted_iota(jnp.int32, (q_rows, steps * rows), 1)
        step_of = lax.broadcasted_iota(jnp.int32, (q_rows, steps * rows), 0) // blocks + g * per
        causal = spot // rows <= step_of
        spot_row = spot % rows

        def one_row(r):
            starts = [pl.multiple_of((t * rows + r) * blocks, blocks) for t in range(per)]
            base = jnp.concatenate([qn[pl.ds(at, blocks), :] for at in starts], axis=0)
            live = far_live[pl.ds(r, 1), :] > 0.5
            near_live = causal & (spot_row == r)
            mixed = None
            for h in range(kv):
                gain = query_gain[h * blocks:(h + 1) * blocks, :]
                query = (base * jnp.concatenate([gain] * per, axis=0)).astype(BF16)
                far = lax.dot_general(
                    query, keys[r, :, cut(h)], contract, preferred_element_type=F32) * scale
                near = lax.dot_general(
                    query, near_k[:, cut(h)], contract, preferred_element_type=F32) * scale
                far = jnp.where(live, far, NEG)
                near = jnp.where(near_live, near, NEG)
                top = jnp.maximum(
                    jnp.max(far, axis=-1, keepdims=True), jnp.max(near, axis=-1, keepdims=True))
                far = jnp.exp(far - top)
                near = jnp.exp(near - top)
                inverse = 1.0 / (
                    jnp.sum(far, axis=-1, keepdims=True) + jnp.sum(near, axis=-1, keepdims=True))
                part_out = jnp.dot(
                    (far * inverse).astype(BF16), values[r, :, cut(h)], preferred_element_type=F32)
                part_out += jnp.dot(
                    (near * inverse).astype(BF16), near_v[:, cut(h)], preferred_element_type=F32)
                mixed = part_out if mixed is None else mixed + part_out
            for t in range(per):
                att[pl.ds(starts[t], blocks), :] = mixed[t * blocks:(t + 1) * blocks, :]

        @pl.loop(0, rows // 4)
        def _(quad):
            for i in range(4):
                one_row(quad * 4 + i)

        square = jnp.zeros((count, head), F32)
        for j in range(blocks):
            piece = h_in[g, :, cut(j)].astype(F32) + att[pl.ds(j, count, stride=blocks), :]
            mid[:, cut(j)] = piece
            square = square + piece * piece
        factor = lax.rsqrt(jnp.sum(square, axis=-1, keepdims=True) / width + EPS)
        for j in range(blocks):
            x_land[g, 0, z, :, cut(j)] = (mid[:, cut(j)] * factor * moe_gain[:, cut(j)]).astype(BF16)

        for k in range(1, nz):
            ag_copy(g, k).start()
        fwd_copy(g, 0).start()
        for k in range(1, nz):
            landed(x_land.at[g, 0, peer(k)], ag_recv.at[g, 0, peer(k)])
            fwd_copy(g, k).start()
        for k in range(nz):
            landed(x_land.at[g, 1, peer(k)], ag_recv.at[g, 1, peer(k)])

        if g == 0:
            for load in loads[2:]:
                load.wait()

        chunk = min(total, 512)
        per_chunk = chunk // count

        for c in range(total // chunk):
            line, first = c * per_chunk // nz, c * per_chunk % nz
            if per_chunk <= nz:
                rows_in = x_land[g, line, first:first + per_chunk].reshape(chunk, width)
            else:
                rows_in = x_land[g].reshape(chunk, width)
            share = shares[g, c * chunk:(c + 1) * chunk, :]

            @pl.loop(0, ff // 256)
            def _(i):
                at = pl.ds(pl.multiple_of(i * 256, 256), 256)
                gate_part = jnp.dot(rows_in, gate[:, at], preferred_element_type=F32)
                lifted = jnp.dot(rows_in, up[:, at], preferred_element_type=F32)
                act[:, at] = (gate_part / (1.0 + jnp.exp(-gate_part)) * lifted).astype(BF16)

            @pl.loop(0, width // 256)
            def _(i):
                at = pl.ds(pl.multiple_of(i * 256, 256), 256)
                served = jnp.dot(act[...], down[:, at], preferred_element_type=F32).astype(BF16)
                term = (served.astype(F32) * share).astype(BF16)
                if per_chunk <= nz:
                    y[g, line, first:first + per_chunk, :, at] = term.reshape(per_chunk, count, 256)
                else:
                    y[g, :, :, :, at] = term.reshape(2, nz, count, 256)

        for k in list(range(1, nz)) + [0]:
            p_copy(g, k).start()
        for k in range(1, nz):
            at = peer(k)
            landed(p_land.at[g, at], p_recv.at[g, at])
            y[g, 0, at] = (y[g, 0, at].astype(F32) + p_land[g, at].astype(F32)).astype(BF16)
            q_copy(g, k).start()
        landed(p_land.at[g, z], p_recv.at[g, z])
        for j in range(blocks):
            piece = y[g, 0, z, :, cut(j)].astype(F32) + p_land[g, z, :, cut(j)].astype(F32)
            mid[:, cut(j)] = mid[:, cut(j)] + piece
        for k in range(1, nz):
            landed(q_land.at[g, peer(k)], q_recv.at[g, peer(k)])
        for j in range(blocks):
            piece = mid[:, cut(j)]
            for k in range(1, nz):
                piece = piece + q_land[g, peer(k), :, cut(j)].astype(F32)
            out[g, :, cut(j)] = piece.astype(BF16)

        @pl.when(sec < last)
        def _():
            h_copy(g).start()

    @pl.when(sec == 0)
    def _():
        landed(emb_land.at[0, pl.ds(0, n_exp - 1)], emb_send)

    @pl.when(sec > 0)
    def _():
        landed(emb_land.at[0], emb_send)

    for g in range(n_groups):
        for k in range(1, nz):
            ag_copy(g, k).wait_send()
            q_copy(g, k).wait_send()
        for k in range(nz):
            fwd_copy(g, k).wait_send()
            p_copy(g, k).wait_send()

        @pl.when(sec < last)
        def _():
            h_copy(g).wait_send()


def on_device(
    token_ids, embed_table, attn_gain, moe_gain, query_gain, key_gain, key_cache, value_cache,
    cache_len, expert_ids, route_raw, gate_weights, up_weights, down_weights,
):
    n_sec = lax.axis_size("section")
    n_exp = lax.axis_size("expert")
    sec = lax.axis_index("section")
    me = lax.axis_index("expert")
    steps, all_rows = token_ids.shape
    vocab_part, part = embed_table.shape
    rows = all_rows // n_exp
    width = attn_gain.shape[1]
    head = query_gain.shape[2]
    kv = key_gain.shape[1]
    blocks = width // head
    cache = key_cache.shape[2]
    ff = gate_weights.shape[3]
    nz = n_exp // 2
    groups = GROUPS
    per = steps // groups
    count = per * rows

    ordered = token_ids.reshape(steps, n_exp, rows).transpose(1, 0, 2).reshape(n_exp, steps * rows)
    shifted = ordered - sec * vocab_part
    inside = (shifted >= 0) & (shifted < vocab_part)
    looked = jnp.take(embed_table, jnp.clip(shifted, 0, vocab_part - 1), axis=0)
    looked = jnp.where(inside[:, :, None], looked, jnp.zeros_like(looked))

    far_live = (jnp.arange(cache)[None, :] < cache_len[:, None]).astype(F32)
    weights = route_raw[0] / jnp.sum(route_raw[0], axis=-1, keepdims=True)
    share = jnp.sum(jnp.where(expert_ids[0] == me, weights, 0.0), axis=-1)
    share = share.reshape(groups, per, nz, 2, rows).transpose(0, 3, 2, 1, 4)
    share = jnp.where(me % 2 == 0, share, share[:, ::-1])
    share = share.reshape(groups, 2 * nz * count, 1)

    dims = (rows, steps, width, head, kv, blocks, ff)
    vmem = pl.BlockSpec(memory_space=pltpu.VMEM)
    hbm = pl.BlockSpec(memory_space=pl.ANY)
    dma = pltpu.SemaphoreType.DMA
    out = pl.pallas_call(
        functools.partial(layers_kernel, n_sec, n_exp, groups, dims),
        out_shape=jax.ShapeDtypeStruct((groups, count, width), BF16),
        in_specs=[vmem] * 7 + [hbm] * 5,
        out_specs=vmem,
        scratch_shapes=[
            pltpu.VMEM(key_cache.shape[1:], BF16),
            pltpu.VMEM(key_cache.shape[1:], BF16),
            pltpu.VMEM((width, ff), BF16),
            pltpu.VMEM((width, ff), BF16),
            pltpu.VMEM((ff, width), BF16),
            pltpu.VMEM((n_sec, n_exp, steps * rows, part), BF16),
            pltpu.VMEM((groups, count, width), BF16),
            pltpu.VMEM((steps * rows, kv * head), BF16),
            pltpu.VMEM((steps * rows, kv * head), BF16),
            pltpu.VMEM((count * blocks, head), F32),
            pltpu.VMEM((count * blocks, head), F32),
            pltpu.VMEM((count, width), F32),
            pltpu.VMEM((groups, 2, nz, count, width), BF16),
            pltpu.VMEM((min(2 * nz * count, 512), ff), BF16),
            pltpu.VMEM((groups, 2, nz, count, width), BF16),
            pltpu.VMEM((groups, nz, count, width), BF16),
            pltpu.VMEM((groups, nz, count, width), BF16),
            dma((5,)), dma, dma, dma((groups,)), dma((groups,)),
            dma((groups, nz)), dma((groups, nz)), dma((groups, 2, nz)),
            dma((groups, nz)), dma((groups, nz)), dma((groups, nz)), dma((groups, nz)),
        ],
        compiler_params=pltpu.CompilerParams(
            collective_id=0, has_side_effects=True, vmem_limit_bytes=60 * 2**20
        ),
    )(
        looked, far_live, share, attn_gain, moe_gain, query_gain[0], key_gain[0],
        key_cache[0], value_cache[0], gate_weights[0, 0], up_weights[0, 0], down_weights[0, 0],
    )
    return out.reshape(1, steps, rows, width)


def solution(mesh):
    in_specs = (
        P(),
        P("section", "expert"),
        P("section", None),
        P("section", None),
        P("section", None, None),
        P("section", None, None),
        P("section", "expert", None, None),
        P("section", "expert", None, None),
        P("expert"),
        P("section", None, None, None),
        P("section", None, None, None),
        P("section", "expert", None, None),
        P("section", "expert", None, None),
        P("section", "expert", None, None),
    )
    out_specs = P("section", None, "expert", None)
    return jax.shard_map(
        on_device, mesh=mesh, in_specs=in_specs, out_specs=out_specs, check_vma=False
    )
```

```python
import functools
import math

import jax
import jax.numpy as jnp
from jax import lax
from jax.experimental import pallas as pl
from jax.experimental.pallas import tpu as pltpu
from jax.sharding import PartitionSpec as P

GROUPS = 4
EPS = 1e-06
NEG = -1e30
MESH = pl.DeviceIdType.MESH
F32 = jnp.float32
BF16 = jnp.bfloat16


def layers_kernel(
    n_sec, n_exp, n_groups, dims,
    looked, far_live, shares, attn_gain, moe_gain, query_gain, key_gain,
    keys_hbm, values_hbm, gate_hbm, up_hbm, down_hbm,
    out,
    keys, values, gate, up, down,
    emb_land, h_in, near_k, near_v, qn, att, mid,
    x_land, act, y, p_land, q_land,
    load_sem, emb_send, emb_recv, h_send, h_recv,
    ag_send, fwd_send, ag_recv, p_send, p_recv, q_send, q_recv,
):
    rows, steps, width, head, kv, blocks, ff, cache = dims
    part = width // n_exp
    nz = n_exp // 2
    per = steps // n_groups
    count = per * rows
    total = 2 * nz * count
    sec = lax.axis_index("section")
    me = lax.axis_index("expert")
    z, x = me // 2, me % 2
    partner = z * 2 + (1 - x)
    last = n_sec - 1

    loads = [
        pltpu.make_async_copy(src, dst, load_sem.at[i])
        for i, (src, dst) in enumerate(
            [(keys_hbm, keys.at[:, 0:cache]), (values_hbm, values.at[:, 0:cache]), (gate_hbm, gate), (up_hbm, up), (down_hbm, down)]
        )
    ]
    for load in loads:
        load.start()

    def peer(k):
        return lax.rem(z + k, nz)

    barrier = pltpu.get_barrier_semaphore()

    def greet(section, expert):
        pl.semaphore_signal(
            barrier, inc=1, device_id={"section": section, "expert": expert}, device_id_type=MESH
        )

    for k in range(1, nz):
        greet(sec, peer(k) * 2 + x)
    greet(sec, partner)

    @pl.when(sec > 0)
    def _():
        greet(sec - 1, me)
        for k in range(n_exp):
            greet(0, k)

    @pl.when(sec < last)
    def _():
        greet(sec + 1, me)

    @pl.when(sec == 0)
    def _():
        for k in range(1, n_exp):
            greet(0, lax.rem(me + k, n_exp))
        for s in range(1, n_sec):
            for k in range(n_exp):
                greet(s, k)

    @pl.when(sec == 0)
    def _():
        pl.semaphore_wait(barrier, nz + n_exp * n_sec)

    @pl.when((sec > 0) & (sec < last))
    def _():
        pl.semaphore_wait(barrier, nz + n_exp + 2)

    @pl.when(sec == last)
    def _():
        pl.semaphore_wait(barrier, nz + n_exp + 1)

    def emb_copy(g, k):
        to = lax.rem(me + k, n_exp)
        return pltpu.make_async_remote_copy(
            src_ref=looked.at[g, to], dst_ref=emb_land.at[g, sec, me],
            send_sem=emb_send.at[g], recv_sem=emb_recv.at[g],
            device_id={"section": 0, "expert": to}, device_id_type=MESH,
        )

    for g in range(n_groups):
        for k in range(1, n_exp):
            emb_copy(g, k).start()

        @pl.when(sec > 0)
        def _():
            emb_copy(g, 0).start()

        @pl.when(sec == 0)
        def _():
            pltpu.make_async_copy(looked.at[g, me], emb_land.at[g, 0, me], emb_recv.at[g]).start()

    near_k[...] = jnp.zeros_like(near_k)
    near_v[...] = jnp.zeros_like(near_v)

    def h_copy(g):
        return pltpu.make_async_remote_copy(
            src_ref=out.at[g], dst_ref=h_in.at[g],
            send_sem=h_send.at[g], recv_sem=h_recv.at[g],
            device_id={"section": sec + 1, "expert": me}, device_id_type=MESH,
        )

    def ag_copy(g, k):
        return pltpu.make_async_remote_copy(
            src_ref=x_land.at[g, 0, z], dst_ref=x_land.at[g, 0, z],
            send_sem=ag_send.at[g, k], recv_sem=ag_recv.at[g, 0, z],
            device_id={"section": sec, "expert": peer(k) * 2 + x}, device_id_type=MESH,
        )

    def fwd_copy(g, k):
        at = peer(k)
        return pltpu.make_async_remote_copy(
            src_ref=x_land.at[g, 0, at], dst_ref=x_land.at[g, 1, at],
            send_sem=fwd_send.at[g, k], recv_sem=ag_recv.at[g, 1, at],
            device_id={"section": sec, "expert": partner}, device_id_type=MESH,
        )

    def p_copy(g, k):
        at = peer(k)
        return pltpu.make_async_remote_copy(
            src_ref=y.at[g, 1, at], dst_ref=p_land.at[g, at],
            send_sem=p_send.at[g, k], recv_sem=p_recv.at[g, at],
            device_id={"section": sec, "expert": partner}, device_id_type=MESH,
        )

    def q_copy(g, k):
        at = peer(k)
        return pltpu.make_async_remote_copy(
            src_ref=y.at[g, 0, at], dst_ref=q_land.at[g, z],
            send_sem=q_send.at[g, k], recv_sem=q_recv.at[g, z],
            device_id={"section": sec, "expert": at * 2 + x}, device_id_type=MESH,
        )

    def landed(ref, sem):
        pltpu.make_async_copy(ref, ref, sem).wait()

    def cut(j, size=head):
        return slice(j * size, (j + 1) * size)

    scale = 1.0 / math.sqrt(head)
    contract = (((1,), (1,)), ((), ()))
    q_rows = per * blocks
    span = cache + 16

    def attention(g):
        @pl.when(sec == 0)
        def _():
            landed(emb_land.at[g], emb_recv.at[g])
            for e in range(n_exp):
                whole = emb_land[g, 0, e].astype(F32)
                for s in range(1, n_sec):
                    whole = whole + emb_land[g, s, e].astype(F32)
                h_in[g, :, e * part:(e + 1) * part] = whole.astype(BF16)

        @pl.when(sec > 0)
        def _():
            landed(h_in.at[g], h_recv.at[g])

        square = jnp.zeros((count, head), F32)
        for j in range(blocks):
            piece = h_in[g, :, cut(j)].astype(F32)
            square = square + piece * piece
        factor = lax.rsqrt(jnp.sum(square, axis=-1, keepdims=True) / width + EPS)
        for j in range(blocks):
            piece = h_in[g, :, cut(j)].astype(F32) * factor * attn_gain[:, cut(j)]
            normed = piece * lax.rsqrt(jnp.mean(piece * piece, axis=-1, keepdims=True) + EPS)
            qn[pl.ds(j, count, stride=blocks), :] = normed
            here = slice(g * count, (g + 1) * count)
            if j < kv:
                near_k[j, here, :] = normed * key_gain[j:j + 1, :]
            elif j < 2 * kv:
                near_v[j - kv, here, :] = piece

        if g == 0:
            loads[0].wait()
            loads[1].wait()

        spot = lax.broadcasted_iota(jnp.int32, (kv * q_rows, span), 1) - cache
        step_of = lax.broadcasted_iota(jnp.int32, (kv * q_rows, span), 0) % q_rows // blocks + g * per
        causal = (spot >= 0) & (spot <= step_of)
        gains = [
            jnp.concatenate([query_gain[h * blocks:(h + 1) * blocks, :]] * per, axis=0)
            for h in range(kv)
        ]
        blank = jnp.zeros((q_rows, head), BF16)
        fill = jnp.zeros((16 - steps, head), F32)

        def near_tile(ref, r):
            return jnp.concatenate(
                [
                    jnp.concatenate([ref[h, pl.ds(r, steps, stride=rows), :], fill], axis=0)
                    for h in range(kv)
                ],
                axis=1,
            ).astype(BF16)

        def one_row(r):
            starts = [pl.multiple_of((t * rows + r) * blocks, blocks) for t in range(per)]
            base = jnp.concatenate([qn[pl.ds(at, blocks), :] for at in starts], axis=0)
            keys[r, cache:span, :] = near_tile(near_k, r)
            values[r, cache:span, :] = near_tile(near_v, r)
            query = jnp.concatenate(
                [
                    jnp.concatenate(
                        [(base * gains[h]).astype(BF16) if i == h else blank for i in range(kv)],
                        axis=1,
                    )
                    for h in range(kv)
                ],
                axis=0,
            )
            live = (far_live[pl.ds(r, 1), :] > 0.5) | causal
            score = lax.dot_general(query, keys[r], contract, preferred_element_type=F32) * scale
            score = jnp.where(live, score, NEG)
            score = jnp.exp(score - jnp.max(score, axis=-1, keepdims=True))
            probs = (score * (1.0 / jnp.sum(score, axis=-1, keepdims=True))).astype(BF16)
            mixed = jnp.dot(probs, values[r], preferred_element_type=F32)
            both = mixed[:q_rows, :head]
            for h in range(1, kv):
                both = both + mixed[h * q_rows:(h + 1) * q_rows, h * head:(h + 1) * head]
            for t in range(per):
                att[pl.ds(starts[t], blocks), :] = both[t * blocks:(t + 1) * blocks, :]

        @pl.loop(0, rows // 8)
        def _(octet):
            for i in range(8):
                one_row(octet * 8 + i)

        square = jnp.zeros((count, head), F32)
        for j in range(blocks):
            piece = h_in[g, :, cut(j)].astype(F32) + att[pl.ds(j, count, stride=blocks), :]
            mid[g, :, cut(j)] = piece
            square = square + piece * piece
        factor = lax.rsqrt(jnp.sum(square, axis=-1, keepdims=True) / width + EPS)
        for j in range(blocks):
            x_land[g, 0, z, :, cut(j)] = (mid[g, :, cut(j)] * factor * moe_gain[:, cut(j)]).astype(BF16)

        for k in range(1, nz):
            ag_copy(g, k).start()
        fwd_copy(g, 0).start()

    def forward(g):
        for k in range(1, nz):
            landed(x_land.at[g, 0, peer(k)], ag_recv.at[g, 0, peer(k)])
            fwd_copy(g, k).start()

    def experts(g):
        for k in range(nz):
            landed(x_land.at[g, 1, peer(k)], ag_recv.at[g, 1, peer(k)])

        if g == 0:
            for load in loads[2:]:
                load.wait()

        rows_in = x_land[g].reshape(total, width)
        share = shares[g]

        @pl.loop(0, ff // 256)
        def _(i):
            at = pl.ds(pl.multiple_of(i * 256, 256), 256)
            gate_part = jnp.dot(rows_in, gate[:, at], preferred_element_type=F32)
            lifted = jnp.dot(rows_in, up[:, at], preferred_element_type=F32)
            act[:, at] = (gate_part / (1.0 + jnp.exp(-gate_part)) * lifted).astype(BF16)

        @pl.loop(0, width // 256)
        def _(i):
            at = pl.ds(pl.multiple_of(i * 256, 256), 256)
            served = jnp.dot(act[...], down[:, at], preferred_element_type=F32).astype(BF16)
            term = (served.astype(F32) * share).astype(BF16)
            y[g, :, :, :, at] = term.reshape(2, nz, count, 256)

        for k in list(range(1, nz)) + [0]:
            p_copy(g, k).start()

    def pair_up(g):
        for k in range(1, nz):
            at = peer(k)
            landed(p_land.at[g, at], p_recv.at[g, at])
            y[g, 0, at] = (y[g, 0, at].astype(F32) + p_land[g, at].astype(F32)).astype(BF16)
            q_copy(g, k).start()

    def finish(g):
        landed(p_land.at[g, z], p_recv.at[g, z])
        for k in range(1, nz):
            landed(q_land.at[g, peer(k)], q_recv.at[g, peer(k)])
        for j in range(blocks):
            piece = y[g, 0, z, :, cut(j)].astype(F32) + p_land[g, z, :, cut(j)].astype(F32)
            for k in range(1, nz):
                piece = piece + q_land[g, peer(k), :, cut(j)].astype(F32)
            out[g, :, cut(j)] = (mid[g, :, cut(j)] + piece).astype(BF16)

        @pl.when(sec < last)
        def _():
            h_copy(g).start()

    attention(0)
    for g in range(n_groups):
        forward(g)
        if g > 0:
            finish(g - 1)
        experts(g)
        if g + 1 < n_groups:
            attention(g + 1)
        pair_up(g)
    finish(n_groups - 1)

    @pl.when(sec == 0)
    def _():
        for g in range(n_groups):
            landed(emb_land.at[g, 0, pl.ds(0, n_exp - 1)], emb_send.at[g])

    @pl.when(sec > 0)
    def _():
        for g in range(n_groups):
            landed(emb_land.at[g, 0], emb_send.at[g])

    for g in range(n_groups):
        for k in range(1, nz):
            ag_copy(g, k).wait_send()
            q_copy(g, k).wait_send()
        for k in range(nz):
            fwd_copy(g, k).wait_send()
            p_copy(g, k).wait_send()

        @pl.when(sec < last)
        def _():
            h_copy(g).wait_send()


def on_device(
    token_ids, embed_table, attn_gain, moe_gain, query_gain, key_gain, key_cache, value_cache,
    cache_len, expert_ids, route_raw, gate_weights, up_weights, down_weights,
):
    n_sec = lax.axis_size("section")
    n_exp = lax.axis_size("expert")
    sec = lax.axis_index("section")
    me = lax.axis_index("expert")
    steps, all_rows = token_ids.shape
    vocab_part, part = embed_table.shape
    rows = all_rows // n_exp
    width = attn_gain.shape[1]
    head = query_gain.shape[2]
    kv = key_gain.shape[1]
    blocks = width // head
    cache = key_cache.shape[2]
    ff = gate_weights.shape[3]
    nz = n_exp // 2
    groups = GROUPS
    per = steps // groups
    count = per * rows

    ordered = token_ids.reshape(groups, per, n_exp, rows).transpose(0, 2, 1, 3)
    ordered = ordered.reshape(groups, n_exp, count)
    shifted = ordered - sec * vocab_part
    inside = (shifted >= 0) & (shifted < vocab_part)
    looked = jnp.take(embed_table, jnp.clip(shifted, 0, vocab_part - 1), axis=0)
    looked = jnp.where(inside[..., None], looked, jnp.zeros_like(looked))

    spots = jnp.arange(cache + 16)[None, :]
    far_live = ((spots < cache) & (spots < cache_len[:, None])).astype(F32)
    weights = route_raw[0] / jnp.sum(route_raw[0], axis=-1, keepdims=True)
    share = jnp.sum(jnp.where(expert_ids[0] == me, weights, 0.0), axis=-1)
    share = share.reshape(groups, per, nz, 2, rows).transpose(0, 3, 2, 1, 4)
    share = jnp.where(me % 2 == 0, share, share[:, ::-1])
    share = share.reshape(groups, 2 * nz * count, 1)

    dims = (rows, steps, width, head, kv, blocks, ff, cache)
    vmem = pl.BlockSpec(memory_space=pltpu.VMEM)
    hbm = pl.BlockSpec(memory_space=pl.ANY)
    dma = pltpu.SemaphoreType.DMA
    out = pl.pallas_call(
        functools.partial(layers_kernel, n_sec, n_exp, groups, dims),
        out_shape=jax.ShapeDtypeStruct((groups, count, width), BF16),
        in_specs=[vmem] * 7 + [hbm] * 5,
        out_specs=vmem,
        scratch_shapes=[
            pltpu.VMEM((rows, cache + 16, kv * head), BF16),
            pltpu.VMEM((rows, cache + 16, kv * head), BF16),
            pltpu.VMEM((width, ff), BF16),
            pltpu.VMEM((width, ff), BF16),
            pltpu.VMEM((ff, width), BF16),
            pltpu.VMEM((groups, n_sec, n_exp, count, part), BF16),
            pltpu.VMEM((groups, count, width), BF16),
            pltpu.VMEM((kv, steps * rows, head), F32),
            pltpu.VMEM((kv, steps * rows, head), F32),
            pltpu.VMEM((count * blocks, head), F32),
            pltpu.VMEM((count * blocks, head), F32),
            pltpu.VMEM((groups, count, width), F32),
            pltpu.VMEM((groups, 2, nz, count, width), BF16),
            pltpu.VMEM((2 * nz * count, ff), BF16),
            pltpu.VMEM((groups, 2, nz, count, width), BF16),
            pltpu.VMEM((groups, nz, count, width), BF16),
            pltpu.VMEM((groups, nz, count, width), BF16),
            dma((5,)), dma((groups,)), dma((groups,)), dma((groups,)), dma((groups,)),
            dma((groups, nz)), dma((groups, nz)), dma((groups, 2, nz)),
            dma((groups, nz)), dma((groups, nz)), dma((groups, nz)), dma((groups, nz)),
        ],
        compiler_params=pltpu.CompilerParams(
            collective_id=0, has_side_effects=True, vmem_limit_bytes=60 * 2**20
        ),
    )(
        looked, far_live, share, attn_gain, moe_gain, query_gain[0], key_gain[0],
        key_cache[0], value_cache[0], gate_weights[0, 0], up_weights[0, 0], down_weights[0, 0],
    )
    return out.reshape(1, steps, rows, width)


def solution(mesh):
    in_specs = (
        P(),
        P("section", "expert"),
        P("section", None),
        P("section", None),
        P("section", None, None),
        P("section", None, None),
        P("section", "expert", None, None),
        P("section", "expert", None, None),
        P("expert"),
        P("section", None, None, None),
        P("section", None, None, None),
        P("section", "expert", None, None),
        P("section", "expert", None, None),
        P("section", "expert", None, None),
    )
    out_specs = P("section", None, "expert", None)
    return jax.shard_map(
        on_device, mesh=mesh, in_specs=in_specs, out_specs=out_specs, check_vma=False
    )
```

```python
import functools
import math

import jax
import jax.numpy as jnp
from jax import lax
from jax.experimental import pallas as pl
from jax.experimental.pallas import tpu as pltpu
from jax.sharding import PartitionSpec as P

GROUPS = 4
EPS = 1e-06
NEG = -1e30
MESH = pl.DeviceIdType.MESH
F32 = jnp.float32
BF16 = jnp.bfloat16


def layers_kernel(
    n_sec, n_exp, n_groups, dims,
    looked, far_live, shares, attn_gain, moe_gain, query_gain, key_gain,
    keys_hbm, values_hbm, gate_hbm, up_hbm, down_hbm,
    out,
    keys, values, gate, up, down,
    emb_land, h_in, near_k, near_v, qn, att, mid,
    x_land, act, y, p_land, q_land,
    load_sem, emb_send, emb_recv, h_send, h_recv,
    ag_send, fwd_send, ag_recv, p_send, p_recv, q_send, q_recv,
):
    rows, steps, width, head, kv, blocks, ff, cache = dims
    part = width // n_exp
    nz = n_exp // 2
    per = steps // n_groups
    count = per * rows
    total = 2 * nz * count
    sec = lax.axis_index("section")
    me = lax.axis_index("expert")
    z, x = me // 2, me % 2
    partner = z * 2 + (1 - x)
    last = n_sec - 1

    loads = [
        pltpu.make_async_copy(src, dst, load_sem.at[i])
        for i, (src, dst) in enumerate(
            [(keys_hbm, keys.at[:, 0:cache]), (values_hbm, values.at[:, 0:cache]), (gate_hbm, gate), (up_hbm, up), (down_hbm, down)]
        )
    ]
    for load in loads:
        load.start()

    def peer(k):
        return lax.rem(z + k, nz)

    barrier = pltpu.get_barrier_semaphore()

    def greet(section, expert):
        pl.semaphore_signal(
            barrier, inc=1, device_id={"section": section, "expert": expert}, device_id_type=MESH
        )

    for k in range(1, nz):
        greet(sec, peer(k) * 2 + x)
    greet(sec, partner)

    @pl.when(sec > 0)
    def _():
        greet(sec - 1, me)
        for k in range(n_exp):
            greet(0, k)

    @pl.when(sec < last)
    def _():
        greet(sec + 1, me)

    @pl.when(sec == 0)
    def _():
        for k in range(1, n_exp):
            greet(0, lax.rem(me + k, n_exp))
        for s in range(1, n_sec):
            for k in range(n_exp):
                greet(s, k)

    @pl.when(sec == 0)
    def _():
        pl.semaphore_wait(barrier, nz + n_exp * n_sec)

    @pl.when((sec > 0) & (sec < last))
    def _():
        pl.semaphore_wait(barrier, nz + n_exp + 2)

    @pl.when(sec == last)
    def _():
        pl.semaphore_wait(barrier, nz + n_exp + 1)

    def emb_copy(g, k):
        to = lax.rem(me + k, n_exp)
        return pltpu.make_async_remote_copy(
            src_ref=looked.at[g, to], dst_ref=emb_land.at[g, sec, me],
            send_sem=emb_send.at[g], recv_sem=emb_recv.at[g],
            device_id={"section": 0, "expert": to}, device_id_type=MESH,
        )

    for g in range(n_groups):
        for k in range(1, n_exp):
            emb_copy(g, k).start()

        @pl.when(sec > 0)
        def _():
            emb_copy(g, 0).start()

        @pl.when(sec == 0)
        def _():
            pltpu.make_async_copy(looked.at[g, me], emb_land.at[g, 0, me], emb_recv.at[g]).start()

    near_k[...] = jnp.zeros_like(near_k)
    near_v[...] = jnp.zeros_like(near_v)

    def h_copy(g):
        return pltpu.make_async_remote_copy(
            src_ref=out.at[g], dst_ref=h_in.at[g],
            send_sem=h_send.at[g], recv_sem=h_recv.at[g],
            device_id={"section": sec + 1, "expert": me}, device_id_type=MESH,
        )

    def ag_copy(g, k):
        return pltpu.make_async_remote_copy(
            src_ref=x_land.at[g, 0, z], dst_ref=x_land.at[g, 0, z],
            send_sem=ag_send.at[g, k], recv_sem=ag_recv.at[g, 0, z],
            device_id={"section": sec, "expert": peer(k) * 2 + x}, device_id_type=MESH,
        )

    def fwd_copy(g, k):
        at = peer(k)
        return pltpu.make_async_remote_copy(
            src_ref=x_land.at[g, 0, at], dst_ref=x_land.at[g, 1, at],
            send_sem=fwd_send.at[g, k], recv_sem=ag_recv.at[g, 1, at],
            device_id={"section": sec, "expert": partner}, device_id_type=MESH,
        )

    def p_copy(g, k):
        at = peer(k)
        return pltpu.make_async_remote_copy(
            src_ref=y.at[g, 1, at], dst_ref=p_land.at[g, at],
            send_sem=p_send.at[g, k], recv_sem=p_recv.at[g, at],
            device_id={"section": sec, "expert": partner}, device_id_type=MESH,
        )

    def q_copy(g, k):
        at = peer(k)
        return pltpu.make_async_remote_copy(
            src_ref=y.at[g, 0, at], dst_ref=q_land.at[g, z],
            send_sem=q_send.at[g, k], recv_sem=q_recv.at[g, z],
            device_id={"section": sec, "expert": at * 2 + x}, device_id_type=MESH,
        )

    def landed(ref, sem):
        pltpu.make_async_copy(ref, ref, sem).wait()

    def cut(j, size=head):
        return slice(j * size, (j + 1) * size)

    scale = 1.0 / math.sqrt(head)
    contract = (((1,), (1,)), ((), ()))
    q_rows = per * blocks
    span = cache + 16

    def attention(g):
        @pl.when(sec == 0)
        def _():
            landed(emb_land.at[g], emb_recv.at[g])
            for e in range(n_exp):
                whole = emb_land[g, 0, e].astype(F32)
                for s in range(1, n_sec):
                    whole = whole + emb_land[g, s, e].astype(F32)
                h_in[g, :, e * part:(e + 1) * part] = whole.astype(BF16)

        @pl.when(sec > 0)
        def _():
            landed(h_in.at[g], h_recv.at[g])

        square = jnp.zeros((count, head), F32)
        for j in range(blocks):
            piece = h_in[g, :, cut(j)].astype(F32)
            square = square + piece * piece
        factor = lax.rsqrt(jnp.sum(square, axis=-1, keepdims=True) / width + EPS)
        for j in range(blocks):
            piece = h_in[g, :, cut(j)].astype(F32) * factor * attn_gain[:, cut(j)]
            normed = piece * lax.rsqrt(jnp.mean(piece * piece, axis=-1, keepdims=True) + EPS)
            qn[pl.ds(j, count, stride=blocks), :] = normed
            here = slice(g * count, (g + 1) * count)
            if j < kv:
                near_k[j, here, :] = normed * key_gain[j:j + 1, :]
            elif j < 2 * kv:
                near_v[j - kv, here, :] = piece

        if g == 0:
            loads[0].wait()
            loads[1].wait()

        spot = lax.broadcasted_iota(jnp.int32, (kv * q_rows, span), 1) - cache
        step_of = lax.broadcasted_iota(jnp.int32, (kv * q_rows, span), 0) % q_rows // blocks + g * per
        causal = (spot >= 0) & (spot <= step_of)
        gains = [
            jnp.concatenate([query_gain[h * blocks:(h + 1) * blocks, :]] * per, axis=0)
            for h in range(kv)
        ]
        blank = jnp.zeros((q_rows, head), BF16)
        fill = jnp.zeros((16 - steps, head), F32)

        def near_tile(ref, r):
            return jnp.concatenate(
                [
                    jnp.concatenate([ref[h, pl.ds(r, steps, stride=rows), :], fill], axis=0)
                    for h in range(kv)
                ],
                axis=1,
            ).astype(BF16)

        def one_row(r):
            starts = [pl.multiple_of((t * rows + r) * blocks, blocks) for t in range(per)]
            base = jnp.concatenate([qn[pl.ds(at, blocks), :] for at in starts], axis=0)
            keys[r, cache:span, :] = near_tile(near_k, r)
            values[r, cache:span, :] = near_tile(near_v, r)
            query = jnp.concatenate(
                [
                    jnp.concatenate(
                        [(base * gains[h]).astype(BF16) if i == h else blank for i in range(kv)],
                        axis=1,
                    )
                    for h in range(kv)
                ],
                axis=0,
            )
            live = (far_live[pl.ds(r, 1), :] > 0.5) | causal
            score = lax.dot_general(query, keys[r], contract, preferred_element_type=F32) * scale
            score = jnp.where(live, score, NEG)
            score = jnp.exp(score - jnp.max(score, axis=-1, keepdims=True))
            probs = (score * (1.0 / jnp.sum(score, axis=-1, keepdims=True))).astype(BF16)
            mixed = jnp.dot(probs, values[r], preferred_element_type=F32)
            both = mixed[:q_rows, :head]
            for h in range(1, kv):
                both = both + mixed[h * q_rows:(h + 1) * q_rows, h * head:(h + 1) * head]
            for t in range(per):
                att[pl.ds(starts[t], blocks), :] = both[t * blocks:(t + 1) * blocks, :]

        @pl.loop(0, rows // 8)
        def _(octet):
            for i in range(8):
                one_row(octet * 8 + i)

        square = jnp.zeros((count, head), F32)
        for j in range(blocks):
            piece = h_in[g, :, cut(j)].astype(F32) + att[pl.ds(j, count, stride=blocks), :]
            mid[g, :, cut(j)] = piece
            square = square + piece * piece
        factor = lax.rsqrt(jnp.sum(square, axis=-1, keepdims=True) / width + EPS)
        for j in range(blocks):
            x_land[g, 0, z, :, cut(j)] = (mid[g, :, cut(j)] * factor * moe_gain[:, cut(j)]).astype(BF16)

        fwd_copy(g, 0).start()
        for k in range(1, nz):
            ag_copy(g, k).start()

    def forward(g):
        for k in range(1, nz):
            at = nz - k
            landed(x_land.at[g, 0, peer(at)], ag_recv.at[g, 0, peer(at)])
            fwd_copy(g, at).start()

    def experts(g):
        for k in range(nz):
            landed(x_land.at[g, 1, peer(k)], ag_recv.at[g, 1, peer(k)])

        if g == 0:
            for load in loads[2:]:
                load.wait()

        rows_in = x_land[g].reshape(total, width)
        share = shares[g]

        @pl.loop(0, ff // 384)
        def _(i):
            at = pl.ds(pl.multiple_of(i * 384, 384), 384)
            gate_part = jnp.dot(rows_in, gate[:, at], preferred_element_type=F32)
            lifted = jnp.dot(rows_in, up[:, at], preferred_element_type=F32)
            act[:, at] = (gate_part / (1.0 + jnp.exp(-gate_part)) * lifted).astype(BF16)

        @pl.loop(0, width // 512)
        def _(i):
            at = pl.ds(pl.multiple_of(i * 512, 512), 512)
            served = jnp.dot(act[...], down[:, at], preferred_element_type=F32).astype(BF16)
            term = (served.astype(F32) * share).astype(BF16)
            y[g, :, :, :, at] = term.reshape(2, nz, count, 512)

        for k in list(range(1, nz)) + [0]:
            p_copy(g, k).start()

    def pair_up(g):
        for k in range(1, nz):
            at = peer(k)
            landed(p_land.at[g, at], p_recv.at[g, at])
            y[g, 0, at] = (y[g, 0, at].astype(F32) + p_land[g, at].astype(F32)).astype(BF16)
            q_copy(g, k).start()

    def finish(g):
        landed(p_land.at[g, z], p_recv.at[g, z])
        for k in range(1, nz):
            landed(q_land.at[g, peer(k)], q_recv.at[g, peer(k)])
        for j in range(blocks):
            piece = y[g, 0, z, :, cut(j)].astype(F32) + p_land[g, z, :, cut(j)].astype(F32)
            for k in range(1, nz):
                piece = piece + q_land[g, peer(k), :, cut(j)].astype(F32)
            out[g, :, cut(j)] = (mid[g, :, cut(j)] + piece).astype(BF16)

        @pl.when(sec < last)
        def _():
            h_copy(g).start()

    attention(0)
    for g in range(n_groups):
        forward(g)
        if g > 0:
            finish(g - 1)
        experts(g)
        if g + 1 < n_groups:
            attention(g + 1)
        pair_up(g)
    finish(n_groups - 1)

    @pl.when(sec == 0)
    def _():
        for g in range(n_groups):
            landed(emb_land.at[g, 0, pl.ds(0, n_exp - 1)], emb_send.at[g])

    @pl.when(sec > 0)
    def _():
        for g in range(n_groups):
            landed(emb_land.at[g, 0], emb_send.at[g])

    for g in range(n_groups):
        for k in range(1, nz):
            ag_copy(g, k).wait_send()
            q_copy(g, k).wait_send()
        for k in range(nz):
            fwd_copy(g, k).wait_send()
            p_copy(g, k).wait_send()

        @pl.when(sec < last)
        def _():
            h_copy(g).wait_send()


def on_device(
    token_ids, embed_table, attn_gain, moe_gain, query_gain, key_gain, key_cache, value_cache,
    cache_len, expert_ids, route_raw, gate_weights, up_weights, down_weights,
):
    n_sec = lax.axis_size("section")
    n_exp = lax.axis_size("expert")
    sec = lax.axis_index("section")
    me = lax.axis_index("expert")
    steps, all_rows = token_ids.shape
    vocab_part, part = embed_table.shape
    rows = all_rows // n_exp
    width = attn_gain.shape[1]
    head = query_gain.shape[2]
    kv = key_gain.shape[1]
    blocks = width // head
    cache = key_cache.shape[2]
    ff = gate_weights.shape[3]
    nz = n_exp // 2
    groups = GROUPS
    per = steps // groups
    count = per * rows

    ordered = token_ids.reshape(groups, per, n_exp, rows).transpose(0, 2, 1, 3)
    ordered = ordered.reshape(groups, n_exp, count)
    shifted = ordered - sec * vocab_part
    inside = (shifted >= 0) & (shifted < vocab_part)
    looked = jnp.take(embed_table, jnp.clip(shifted, 0, vocab_part - 1), axis=0)
    looked = jnp.where(inside[..., None], looked, jnp.zeros_like(looked))

    spots = jnp.arange(cache + 16)[None, :]
    far_live = ((spots < cache) & (spots < cache_len[:, None])).astype(F32)
    weights = route_raw[0] / jnp.sum(route_raw[0], axis=-1, keepdims=True)
    share = jnp.sum(jnp.where(expert_ids[0] == me, weights, 0.0), axis=-1)
    share = share.reshape(groups, per, nz, 2, rows).transpose(0, 3, 2, 1, 4)
    share = jnp.where(me % 2 == 0, share, share[:, ::-1])
    share = share.reshape(groups, 2 * nz * count, 1)

    dims = (rows, steps, width, head, kv, blocks, ff, cache)
    vmem = pl.BlockSpec(memory_space=pltpu.VMEM)
    hbm = pl.BlockSpec(memory_space=pl.ANY)
    dma = pltpu.SemaphoreType.DMA
    out = pl.pallas_call(
        functools.partial(layers_kernel, n_sec, n_exp, groups, dims),
        out_shape=jax.ShapeDtypeStruct((groups, count, width), BF16),
        in_specs=[vmem] * 7 + [hbm] * 5,
        out_specs=vmem,
        scratch_shapes=[
            pltpu.VMEM((rows, cache + 16, kv * head), BF16),
            pltpu.VMEM((rows, cache + 16, kv * head), BF16),
            pltpu.VMEM((width, ff), BF16),
            pltpu.VMEM((width, ff), BF16),
            pltpu.VMEM((ff, width), BF16),
            pltpu.VMEM((groups, n_sec, n_exp, count, part), BF16),
            pltpu.VMEM((groups, count, width), BF16),
            pltpu.VMEM((kv, steps * rows, head), F32),
            pltpu.VMEM((kv, steps * rows, head), F32),
            pltpu.VMEM((count * blocks, head), F32),
            pltpu.VMEM((count * blocks, head), F32),
            pltpu.VMEM((groups, count, width), F32),
            pltpu.VMEM((groups, 2, nz, count, width), BF16),
            pltpu.VMEM((2 * nz * count, ff), BF16),
            pltpu.VMEM((groups, 2, nz, count, width), BF16),
            pltpu.VMEM((groups, nz, count, width), BF16),
            pltpu.VMEM((groups, nz, count, width), BF16),
            dma((5,)), dma((groups,)), dma((groups,)), dma((groups,)), dma((groups,)),
            dma((groups, nz)), dma((groups, nz)), dma((groups, 2, nz)),
            dma((groups, nz)), dma((groups, nz)), dma((groups, nz)), dma((groups, nz)),
        ],
        compiler_params=pltpu.CompilerParams(
            collective_id=0, has_side_effects=True, vmem_limit_bytes=60 * 2**20
        ),
    )(
        looked, far_live, share, attn_gain, moe_gain, query_gain[0], key_gain[0],
        key_cache[0], value_cache[0], gate_weights[0, 0], up_weights[0, 0], down_weights[0, 0],
    )
    return out.reshape(1, steps, rows, width)


def solution(mesh):
    in_specs = (
        P(),
        P("section", "expert"),
        P("section", None),
        P("section", None),
        P("section", None, None),
        P("section", None, None),
        P("section", "expert", None, None),
        P("section", "expert", None, None),
        P("expert"),
        P("section", None, None, None),
        P("section", None, None, None),
        P("section", "expert", None, None),
        P("section", "expert", None, None),
        P("section", "expert", None, None),
    )
    out_specs = P("section", None, "expert", None)
    return jax.shard_map(
        on_device, mesh=mesh, in_specs=in_specs, out_specs=out_specs, check_vma=False
    )
```
